512 devices in a mesh: tile: 128 (over y, x, z_hi), src: 4 (over z_lo, core).
Axes of the slice: x: 4, y: 8, z: 8 (z_hi: 4, z_lo: 2; z = z_hi * 2 + z_lo), core: 2. Of those that a mesh axis runs over, the one named last changes fastest.
Arguments:
- mask_tiles: int32 [2048, 512], P('tile'), may hold values 0 or 1
- kernels: bfloat16 [16, 3, 8, 2, 17, 17], P('src'), may hold values from -0.5 to 0.5
- source_weight: int32 [16], P('src'), may hold values from 1 to 8
- dill_rate: float32 [8], P('src'), may hold values from 0.3 to 3
- quencher_load: float32 [8], P('src'), may hold values from 0.1 to 0.5
Outputs:
- acid_field: float32 [8, 2048, 512], P('src', 'tile')
- inhibitor: float32 [8, 2048, 512], P('src', 'tile')
The draws below stay inside these ranges and needn't reach their ends.
All inputs are finite; a program needn't handle non-finite values. No bound on the sum of `mask_tiles` on one device may be relied on, other than what follows from the above.
Results may differ from the reference program's by a relative error of at most 0.0008.
Values may be sent and summed in bfloat16 or wider, within the bound.
No kernel may reach another device: no remote copies, remote signals or barrier semaphores. Data moves between devices by JAX's collectives and lax.ppermute only.
A program may use at most 64 MiB of HBM per device.

```python
import math
import jax
import jax.numpy as jnp
from jax import lax

COLS = 512
KS = 17
DEPTH = 8
STEPS = 8
SOURCES = 16
NROWS = 2048


def set_ends(drawn, stream_key, low, high):
    place = [jax.random.randint(jax.random.fold_in(stream_key, axis), (), 0, length) for axis, length in enumerate(drawn.shape)]
    main_axis = drawn.shape.index(max(drawn.shape))
    next_to = place[:main_axis] + [(place[main_axis] + 1) % drawn.shape[main_axis]] + place[main_axis + 1:]
    return drawn.at[tuple(place)].set(low).at[tuple(next_to)].set(high)


def block_levels(stream_key, dims, pieces, low, largest):
    factor_of = 1.0
    for axis_at, parts in pieces:
        heights = jax.random.uniform(jax.random.fold_in(jax.random.fold_in(stream_key, 6), axis_at), (parts,), jnp.float32, low / len(pieces), largest / len(pieces))
        factor_of = factor_of * jnp.repeat(jnp.exp(heights), dims[axis_at] // parts).reshape((-1,) + (1,) * (len(dims) - 1 - axis_at))
    return factor_of


def gaussian(stream_key, extent, deviation, bound, pieces=(), held_as=jnp.bfloat16):
    result = deviation * jax.random.normal(stream_key, extent, jnp.float32)
    if pieces:
        result = result * block_levels(stream_key, extent, pieces, -0.22, 0.18)
    return jnp.clip(result, -bound, bound).astype(held_as)


def setup_inputs(seed: int = 0) -> dict:
    streams_of = jax.random.split(jax.random.key(seed), 6)
    return {
        "mask_tiles": set_ends((jax.random.randint(streams_of[0], (NROWS, COLS), 0, 2) < 1).astype(jnp.int32), jax.random.fold_in(streams_of[0], 1), 0, 1),
        "kernels": gaussian(streams_of[1], (SOURCES, 3, DEPTH, 2, KS, KS), (KS * KS // 2) ** -0.5, 0.5, ((0, 4),)),
        "source_weight": set_ends(jax.random.randint(streams_of[2], (SOURCES,), 1, 9), jax.random.fold_in(streams_of[2], 1), 1, 8).astype(jnp.int32),
        "dill_rate": jnp.clip(jnp.exp(math.log(3.0) - 2.3025851 * jax.random.uniform(streams_of[3], (DEPTH,), jnp.float32) ** block_levels(streams_of[3], (DEPTH,), ((0, 4),), -0.2, 0.2)), 0.3, 3.0),
        "quencher_load": jnp.clip(0.1 + 0.4 * jax.random.uniform(streams_of[4], (DEPTH,), jnp.float32) ** block_levels(streams_of[4], (DEPTH,), ((0, 4),), -0.2, 0.2), 0.1, 0.5),
    }


acid_lateral = 0.15
acid_vertical = 0.12
quench_lateral = 0.05
quench_vertical = 0.04
react_rate = 0.3
deprotect_rate = 0.25


def advance(extended):
    centre = extended[:, 1:-1, 1:-1]
    padded_cols = jnp.pad(centre, ((0, 0), (0, 0), (0, 0), (1, 1)))
    lateral = extended[:, 1:-1, 2:] + extended[:, 1:-1, :-2] + padded_cols[..., 2:] + padded_cols[..., :-2] - 4.0 * centre
    vertical = extended[:, 2:, 1:-1] + extended[:, :-2, 1:-1] - 2.0 * centre
    acid_now = centre[0]
    quench_now = centre[1]
    reacted = react_rate * acid_now * quench_now
    acid_next = acid_now + acid_lateral * lateral[0] + acid_vertical * vertical[0] - reacted
    quench_next = quench_now + quench_lateral * lateral[1] + quench_vertical * vertical[1] - reacted
    return jnp.stack([acid_next, quench_next])


def reference(mask_tiles, kernels, source_weight, dill_rate, quencher_load):
    rim_width = KS // 2
    binary = mask_tiles.astype(jnp.bfloat16)
    padded = jnp.pad(binary, ((rim_width, rim_width), (rim_width, rim_width)))
    frame_band = padded[None, None]

    def one_source(running, source_item):
        kernel_block, weight_value = source_item
        filters = kernel_block.reshape(3 * DEPTH * 2, 1, KS, KS)
        fields = lax.conv_general_dilated(frame_band, filters, (1, 1), "VALID", preferred_element_type=jnp.float32)[0]
        squares = (fields * fields).reshape(3, DEPTH, 2, NROWS, COLS).sum(axis=(0, 2))
        return running + weight_value.astype(jnp.float32) * squares, None

    start_value = jnp.zeros((DEPTH, NROWS, COLS), jnp.float32)
    summed = lax.scan(one_source, start_value, (kernels, source_weight))[0]
    intensity = summed * (1.0 / (24.0 * SOURCES))
    acid_start = 1.0 - jnp.exp(-dill_rate[:, None, None] * intensity)
    quench_start = jnp.broadcast_to(quencher_load[:, None, None], acid_start.shape)
    bake_state = jnp.stack([acid_start, quench_start])
    dose_sum = jnp.zeros_like(acid_start)
    for substep in range(STEPS):
        row_padded = jnp.pad(bake_state, ((0, 0), (0, 0), (1, 1), (0, 0)))
        extended = jnp.concatenate([row_padded[:, :1], row_padded, row_padded[:, -1:]], axis=1)
        bake_state = advance(extended)
        dose_sum = dose_sum + bake_state[0]
    inhibitor = jnp.exp(-deprotect_rate * dose_sum)
    return bake_state[0], inhibitor
```

```python
import jax
import jax.numpy as jnp
from jax import lax
from jax.experimental import pallas as pl
from jax.experimental.pallas import tpu as pltpu
from jax.sharding import PartitionSpec as P

STEPS = 8
KS = 17
TAPS = KS * KS
KPAD = 304
WCOL = 304
WLANES = 384
COLS = 512
TILES = COLS // 128
OWN = 16
ROWS = OWN + 2 * STEPS
BAND = ROWS + KS - 1
PLANES = 8

acid_lateral = 0.15
acid_vertical = 0.12
quench_lateral = 0.05
quench_vertical = 0.04
react_rate = 0.3
deprotect_rate = 0.25


def image_kernel(up_ref, mask_ref, down_ref, w_ref, out_ref, x_ref, b_ref, i_ref):
    f32 = jnp.float32
    x_ref[...] = jnp.zeros_like(x_ref)
    x_ref[0:16, 128:640] = up_ref[...].astype(f32)
    x_ref[16:32, 128:640] = mask_ref[...].astype(f32)
    x_ref[32:48, 128:640] = down_ref[...].astype(f32)
    filled = BAND * KS
    b_ref[:, filled:, :] = jnp.zeros((TILES, b_ref.shape[1] - filled, 128), f32)
    for b in range(KS):
        for t in range(TILES):
            start = 120 + b + 128 * t
            b_ref[t, pl.ds(b, BAND, stride=KS), :] = x_ref[:, start : start + 128]
    w_all = w_ref[...].reshape(192, WLANES)
    weight = w_all[:, WCOL : WCOL + 1].astype(f32)
    w_taps = w_all[:, :KPAD]

    def body(q, carry):
        base = pl.multiple_of(q * (8 * KS), 8)
        view = b_ref.at[:, pl.ds(base, 440), :]
        for d in range(8):
            patches = jnp.concatenate(
                [view[t, KS * d : KS * d + KPAD, :] for t in range(TILES)], axis=1
            ).astype(jnp.bfloat16)
            field = jnp.dot(w_taps, patches, preferred_element_type=f32)
            power = (field * field * weight).reshape(4, 2, 3, 8, COLS)
            total = power.sum(axis=(0, 2)).sum(axis=1)
            for k in range(2):
                i_ref[k, pl.ds(q * 8 + d, 1), :] = total[k : k + 1]
        return carry

    lax.fori_loop(0, ROWS // 8, body, 0)
    out_ref[...] = i_ref[...].astype(jnp.bfloat16)


def bake_kernel(scale, g_ref, w_ref, acid_ref, inhib_ref, a_ref, q_ref, d_ref):
    f32 = jnp.float32
    tile = lax.axis_index("tile")
    src = lax.axis_index("src")
    has_up = jnp.where(tile > 0, 1.0, 0.0).astype(f32)
    has_down = jnp.where(tile < lax.axis_size("tile") - 1, 1.0, 0.0).astype(f32)
    par = w_ref[0, 0:16, :].astype(f32)
    for s in range(1, 4):
        par = par + w_ref[s, 0:16, :].astype(f32)
    par = par[0:8]

    def column(first):
        return par[:, first : first + 1] + par[:, first + 1 : first + 2] + par[:, first + 2 : first + 3]

    dill = jnp.broadcast_to(column(WCOL + 1) * scale, (8, 128))
    quench = jnp.broadcast_to(column(WCOL + 4), (8, 128))
    for k in range(PLANES):
        plane = g_ref[k // 2, k % 2].astype(f32)
        for t in range(TILES):
            a_ref[0, t, pl.ds(k, ROWS, stride=PLANES), :] = plane[:, 128 * t : 128 * t + 128]
    for r in range(ROWS):
        for t in range(TILES):
            cut = slice(8 * r, 8 * r + 8)
            acid = 1.0 - jnp.exp(-dill * a_ref[0, t, cut, :])
            load = quench
            if r < STEPS:
                acid, load = acid * has_up, load * has_up
            elif r >= STEPS + OWN:
                acid, load = acid * has_down, load * has_down
            a_ref[0, t, cut, :] = acid
            q_ref[0, t, cut, :] = load

    lane = lax.broadcasted_iota(jnp.int32, (8, 128), 1)
    sub = lax.broadcasted_iota(jnp.int32, (8, 128), 0)
    first_lane, last_lane = lane == 0, lane == 127
    first_sub, last_sub = sub == 0, sub == 7
    zero = jnp.zeros((8, 128), f32)

    def spread(ref, now, r):
        def rows(at):
            start = pl.multiple_of(at * 8, 8)
            return [ref[now, t, pl.ds(start, 8), :] for t in range(TILES)]

        above, here, below = rows(r - 1), rows(r), rows(r + 1)
        right = [pltpu.roll(v, 1, 1) for v in here]
        left = [pltpu.roll(v, 127, 1) for v in here]
        lateral, vertical = [], []
        for t in range(TILES):
            before = right[t - 1] if t > 0 else zero
            after = left[t + 1] if t < TILES - 1 else zero
            side = jnp.where(first_lane, before, right[t]) + jnp.where(last_lane, after, left[t])
            lateral.append(side + (above[t] + below[t]))
            lower = jnp.where(first_sub, here[t], pltpu.roll(here[t], 1, 0))
            upper = jnp.where(last_sub, here[t], pltpu.roll(here[t], 7, 0))
            vertical.append(lower + upper)
        return here, lateral, vertical

    acid_keep = 1.0 - 4.0 * acid_lateral - 2.0 * acid_vertical
    quench_keep = 1.0 - 4.0 * quench_lateral - 2.0 * quench_vertical
    for step in range(STEPS):
        now, later = step % 2, (step + 1) % 2
        first, last = step + 1, ROWS - 1 - step

        def body(r, carry):
            acid, acid_side, acid_up = spread(a_ref, now, r)
            load, load_side, load_up = spread(q_ref, now, r)
            keep = jnp.where(r < STEPS, has_up, jnp.where(r >= STEPS + OWN, has_down, 1.0))
            start = pl.multiple_of(r * 8, 8)
            for t in range(TILES):
                reacted = (react_rate * acid[t]) * load[t]
                new_acid = acid_keep * acid[t] + acid_lateral * acid_side[t] + acid_vertical * acid_up[t] - reacted
                new_load = quench_keep * load[t] + quench_lateral * load_side[t] + quench_vertical * load_up[t] - reacted
                new_acid = new_acid * keep
                a_ref[later, t, pl.ds(start, 8), :] = new_acid
                q_ref[later, t, pl.ds(start, 8), :] = new_load * keep
                if step == 0:
                    d_ref[t, pl.ds(start, 8), :] = new_acid
                else:
                    d_ref[t, pl.ds(start, 8), :] = d_ref[t, pl.ds(start, 8), :] + new_acid
            return carry

        lax.fori_loop(first, last, body, 0, unroll=2)

    end = STEPS % 2
    for s in range(4):

        @pl.when(src == s)
        def _():
            for k in range(2):
                rows = pl.ds(8 * STEPS + 2 * s + k, OWN, stride=PLANES)
                for t in range(TILES):
                    cut = slice(128 * t, 128 * t + 128)
                    acid_ref[k, :, cut] = a_ref[end, t, rows, :]
                    inhib_ref[k, :, cut] = jnp.exp(-deprotect_rate * d_ref[t, rows, :])


def pieces(x):
    out, rest = [], x
    for _ in range(3):
        part = lax.reduce_precision(rest, 8, 7)
        out.append(part.astype(jnp.bfloat16))
        rest = rest - part
    return out


def shards(mask_tiles, kernels, source_weight, dill_rate, quencher_load):
    bf16 = jnp.bfloat16
    tiles = lax.axis_size("tile")
    sources = kernels.shape[0]
    up = lax.ppermute(mask_tiles, "tile", [(i, i + 1) for i in range(tiles - 1)])
    down = lax.ppermute(mask_tiles, "tile", [(i + 1, i) for i in range(tiles - 1)])

    taps = kernels.reshape(sources, 3, 4, 2, 2, KS, KS).transpose(2, 3, 0, 1, 4, 5, 6).reshape(4, 48, TAPS)
    weight = jnp.broadcast_to(source_weight.astype(bf16)[None, None, :, None], (4, 2, sources, 6)).reshape(4, 48, 1)
    position = lax.axis_index("src") * 2
    values = jnp.stack(pieces(dill_rate) + pieces(quencher_load), axis=1)
    values = lax.dynamic_update_slice(jnp.zeros((48, 6), bf16), values, (position, 0))
    values = jnp.broadcast_to(values[None], (4, 48, 6))
    rest = WLANES - WCOL - 7
    packed = jnp.concatenate(
        [taps, jnp.zeros((4, 48, WCOL - TAPS), bf16), weight, values, jnp.zeros((4, 48, rest), bf16)], axis=2
    )
    w_own = lax.all_to_all(packed, "src", 0, 0)

    intensity = pl.pallas_call(
        image_kernel,
        out_shape=jax.ShapeDtypeStruct((2, ROWS, COLS), bf16),
        scratch_shapes=[
            pltpu.VMEM((BAND, COLS + 256), jnp.float32),
            pltpu.VMEM((TILES, 848, 128), jnp.float32),
            pltpu.VMEM((2, ROWS, COLS), jnp.float32),
        ],
        compiler_params=pltpu.CompilerParams(vmem_limit_bytes=32 * 1024 * 1024),
        name="image",
    )(up, mask_tiles, down, w_own)
    gathered = lax.all_gather(intensity, "src")
    scale = 1.0 / (24.0 * sources * lax.axis_size("src"))

    def bake(*refs):
        bake_kernel(scale, *refs)

    out = jax.ShapeDtypeStruct((2, OWN, COLS), jnp.float32)
    acid, inhibitor = pl.pallas_call(
        bake,
        out_shape=(out, out),
        scratch_shapes=[
            pltpu.VMEM((2, TILES, ROWS * PLANES, 128), jnp.float32),
            pltpu.VMEM((2, TILES, ROWS * PLANES, 128), jnp.float32),
            pltpu.VMEM((TILES, ROWS * PLANES, 128), jnp.float32),
        ],
        compiler_params=pltpu.CompilerParams(vmem_limit_bytes=32 * 1024 * 1024),
        name="bake",
    )(gathered, w_own)
    return acid, inhibitor


def solution(mesh):
    in_specs = (
        P("tile", None),
        P("src", None, None, None, None, None),
        P("src"),
        P("src"),
        P("src"),
    )
    out_specs = (P("src", "tile", None), P("src", "tile", None))
    return jax.shard_map(shards, mesh=mesh, in_specs=in_specs, out_specs=out_specs, check_vma=False)
```

```python
import jax
import jax.numpy as jnp
from jax import lax
from jax.experimental import pallas as pl
from jax.experimental.pallas import tpu as pltpu
from jax.sharding import PartitionSpec as P

STEPS = 8
KS = 17
TAPS = KS * KS
KPAD = 304
WCOL = 304
WLANES = 384
COLS = 512
TILES = COLS // 128
OWN = 16
HALF = 16
ROWS = OWN + 2 * STEPS
PLANES = 8
GROUPS = 4
PARAMS = 64

acid_lateral = 0.15
acid_vertical = 0.12
quench_lateral = 0.05
quench_vertical = 0.04
react_rate = 0.3
deprotect_rate = 0.25


def one_hot(axis):
    place = lax.broadcasted_iota(jnp.int32, (COLS, COLS), 1 - axis)
    column = lax.broadcasted_iota(jnp.int32, (COLS, COLS), axis)
    where_to = (place & 127) * TILES + (place >> 7)
    return jnp.where(where_to == column, 1.0, 0.0).astype(jnp.bfloat16)


def image_kernel(near_ref, mask_ref, w_ref, dill_ref, load_ref, out_ref, b_ref, i_ref):
    f32 = jnp.float32
    upper = lax.axis_index("src") < 2
    near, own = near_ref[...], mask_ref[...]
    band = jnp.concatenate([jnp.where(upper, near, own), jnp.where(upper, own, near)], axis=0)
    band = jnp.dot(band.astype(f32).astype(jnp.bfloat16), one_hot(0), preferred_element_type=f32)
    filled = 2 * HALF * KS
    b_ref[:, filled:, :] = jnp.zeros((TILES, b_ref.shape[1] - filled, 128), f32)
    lane = lax.broadcasted_iota(jnp.int32, (2 * HALF, 128), 1)
    moved = {}
    for m in range(-8, 12):
        tile, by = m % TILES, m // TILES
        block = band[:, 128 * tile : 128 * tile + 128]
        if by:
            block = pltpu.roll(block, (-by) % 128, 1)
            block = jnp.where((lane + by >= 0) & (lane + by < 128), block, 0.0)
        moved[m] = block
    for b in range(KS):
        for t in range(TILES):
            b_ref[t, pl.ds(b, 2 * HALF, stride=KS), :] = moved[t + b - 8]
    w_all = w_ref[...].reshape(384, WLANES)
    weight = w_all[:, WCOL : WCOL + 1].astype(f32)
    w_taps = w_all[:, :KPAD]

    def body(q, carry):
        base = pl.multiple_of(q * (8 * KS), 8)
        view = b_ref.at[:, pl.ds(base, 424), :]
        for d in range(8):
            patches = jnp.concatenate(
                [view[t, KS * d : KS * d + KPAD, :] for t in range(TILES)], axis=1
            ).astype(jnp.bfloat16)
            field = jnp.dot(w_taps, patches, preferred_element_type=f32)
            power = (field * field * weight).reshape(4, 4, 3, 8, COLS)
            total = power.sum(axis=(0, 2)).sum(axis=1)
            for k in range(4):
                at = k * HALF + (d % 4) * 4 + d // 4 + 2 * q
                i_ref[pl.ds(at, 1), :] = total[k : k + 1]
        return carry

    lax.fori_loop(0, HALF // 8, body, 0)
    i_ref[PARAMS:, :] = jnp.zeros((16, COLS), f32)
    at = PARAMS
    for ref in (dill_ref, load_ref):
        for k in range(2):
            rest = jnp.full((1, COLS), ref[k], f32)
            for _ in range(3):
                part = rest.astype(jnp.bfloat16).astype(f32)
                i_ref[at : at + 1, :] = part
                rest = rest - part
                at += 1
    out_ref[...] = i_ref[...].astype(jnp.bfloat16)


def bake_kernel(scale, g_ref, acid_ref, inhib_ref, a_ref, q_ref, d_ref):
    f32 = jnp.float32
    tile = lax.axis_index("tile")
    src = lax.axis_index("src")
    lane = lax.broadcasted_iota(jnp.int32, (8, 128), 1)
    sub = lax.broadcasted_iota(jnp.int32, (8, 128), 0)
    has_up = jnp.where(tile > 0, 1.0, 0.0).astype(f32)
    has_down = jnp.where(tile < lax.axis_size("tile") - 1, 1.0, 0.0).astype(f32)
    keep = jnp.where(sub < 2, has_up, jnp.where(sub >= 6, has_down, 1.0))
    top = sub < 4
    for k in range(PLANES):
        par = g_ref[k // 2, PARAMS : PARAMS + 16, 0:128].astype(f32)

        def constant(at):
            return jnp.broadcast_to(par[at : at + 1] + par[at + 1 : at + 2] + par[at + 2 : at + 3], (8, 128))

        dill = constant(3 * (k % 2)) * -scale
        load = constant(6 + 3 * (k % 2)) * keep
        first = (k % 4) * HALF
        for t in range(TILES):
            cut = slice(128 * t, 128 * t + 128)
            high = g_ref[k // 4, first : first + HALF, cut].astype(f32)
            low = g_ref[k // 4 + 2, first : first + HALF, cut].astype(f32)
            for half in range(2):
                one, two = high[8 * half : 8 * half + 8], low[8 * half : 8 * half + 8]
                pair = (jnp.where(top, one, pltpu.roll(two, 4, 0)), jnp.where(top, pltpu.roll(one, 4, 0), two))
                for i in range(2):
                    at = (2 * half + i) * TILES + t
                    a_ref[0, k, at] = (1.0 - jnp.exp(dill * pair[i])) * keep
                    q_ref[0, k, at] = load

    not_first, not_last = lane > 0, lane < 127
    acid_keep = keep * (1.0 - 4.0 * acid_lateral - 2.0 * acid_vertical)
    load_keep = keep * (1.0 - 4.0 * quench_lateral - 2.0 * quench_vertical)
    acid_side, acid_up = keep * acid_lateral, keep * acid_vertical
    load_side, load_up = keep * quench_lateral, keep * quench_vertical
    react = keep * react_rate

    def around(ref, now, k, here):
        under, over = jnp.maximum(k - 1, 0), jnp.minimum(k + 1, PLANES - 1)
        side, vertical = [], []
        for u in range(GROUPS):
            for t in range(TILES):
                at = u * TILES + t
                above = here[at - TILES] if u > 0 else pltpu.roll(here[at + 3 * TILES], 1, 0)
                below = here[at + TILES] if u < GROUPS - 1 else pltpu.roll(here[at - 3 * TILES], 7, 0)
                left = here[at - 1] if t > 0 else jnp.where(not_first, pltpu.roll(here[at + 3], 1, 1), 0.0)
                right = here[at + 1] if t < TILES - 1 else jnp.where(not_last, pltpu.roll(here[at - 3], 127, 1), 0.0)
                side.append((above + below) + (left + right))
                vertical.append(ref[now, under, at] + ref[now, over, at])
        return side, vertical

    for step in range(STEPS):
        now, later = step % 2, (step + 1) % 2
        reach = STEPS - 1 - step

        def body(k, carry):
            acid = [a_ref[now, k, at] for at in range(16)]
            load = [q_ref[now, k, at] for at in range(16)]
            a_side, a_up = around(a_ref, now, k, acid)
            q_side, q_up = around(q_ref, now, k, load)
            for at in range(16):
                reacted = (react * acid[at]) * load[at]
                a_ref[later, k, at] = (acid_keep * acid[at] + acid_side * a_side[at]) + (acid_up * a_up[at] - reacted)
                q_ref[later, k, at] = (load_keep * load[at] + load_side * q_side[at]) + (load_up * q_up[at] - reacted)
            return carry

        lax.fori_loop(jnp.maximum(2 * src - reach, 0), jnp.minimum(2 * src + 1 + reach, PLANES - 1) + 1, body, 0)
        for k in range(2):
            for at in range(16):
                value = a_ref[later, 2 * src + k, at]
                d_ref[k, at] = value if step == 0 else d_ref[k, at] + value

    end = STEPS % 2
    blocks = []
    for k in range(2):
        for u in range(GROUPS):
            blocks.append(jnp.concatenate([a_ref[end, 2 * src + k, u * TILES + t] for t in range(TILES)], axis=1))
    for k in range(2):
        for u in range(GROUPS):
            blocks.append(jnp.concatenate([d_ref[k, u * TILES + t] for t in range(TILES)], axis=1))
    rest = jnp.concatenate(blocks, axis=0)
    back = one_hot(1)
    result = None
    for _ in range(3):
        part = rest.astype(jnp.bfloat16)
        rest = rest - part.astype(f32)
        moved = jnp.dot(part, back, preferred_element_type=f32)
        result = moved if result is None else result + moved
    inhibitor = jnp.exp(-deprotect_rate * result[64:])
    for k in range(2):
        for u in range(GROUPS):
            for j in range(2, 6):
                row = 32 * k + 8 * u + j
                to = 4 * (j - 2) + u
                acid_ref[k, to : to + 1, :] = result[row : row + 1]
                inhib_ref[k, to : to + 1, :] = inhibitor[row : row + 1]


def shards(mask_tiles, kernels, source_weight, dill_rate, quencher_load):
    bf16 = jnp.bfloat16
    tiles, parts = lax.axis_size("tile"), lax.axis_size("src")
    sources = kernels.shape[0]
    moves = []
    for i in range(tiles - 1):
        for s in range(parts):
            one, two = i * parts + s, (i + 1) * parts + s
            moves.append((one, two) if s < 2 else (two, one))
    near = lax.ppermute(mask_tiles, ("tile", "src"), moves)

    taps = kernels.reshape(sources, 3, 2, 4, 2, KS, KS).transpose(2, 3, 0, 1, 4, 5, 6).reshape(2, 96, TAPS)
    weight = jnp.broadcast_to(source_weight.astype(bf16)[None, None, :, None], (2, 4, sources, 6)).reshape(2, 96, 1)
    packed = jnp.concatenate(
        [taps, jnp.zeros((2, 96, WCOL - TAPS), bf16), weight, jnp.zeros((2, 96, WLANES - WCOL - 1), bf16)], axis=2
    )
    w_own = lax.all_to_all(jnp.concatenate([packed, packed], axis=0), "src", 0, 0)

    smem = pl.BlockSpec(memory_space=pltpu.SMEM)
    vmem = pl.BlockSpec(memory_space=pltpu.VMEM)
    intensity = pl.pallas_call(
        image_kernel,
        out_shape=jax.ShapeDtypeStruct((PARAMS + 16, COLS), bf16),
        in_specs=[vmem, vmem, vmem, smem, smem],
        scratch_shapes=[
            pltpu.VMEM((TILES, 560, 128), jnp.float32),
            pltpu.VMEM((PARAMS + 16, COLS), jnp.float32),
        ],
        compiler_params=pltpu.CompilerParams(vmem_limit_bytes=32 * 1024 * 1024),
        name="image",
    )(near, mask_tiles, w_own, dill_rate, quencher_load)
    gathered = lax.all_gather(intensity, "src")
    scale = 1.0 / (24.0 * sources * parts)

    def bake(*refs):
        bake_kernel(scale, *refs)

    out = jax.ShapeDtypeStruct((2, OWN, COLS), jnp.float32)
    acid, inhibitor = pl.pallas_call(
        bake,
        out_shape=(out, out),
        scratch_shapes=[
            pltpu.VMEM((2, PLANES, 16, 8, 128), jnp.float32),
            pltpu.VMEM((2, PLANES, 16, 8, 128), jnp.float32),
            pltpu.VMEM((2, 16, 8, 128), jnp.float32),
        ],
        compiler_params=pltpu.CompilerParams(vmem_limit_bytes=32 * 1024 * 1024),
        name="bake",
    )(gathered)
    return acid, inhibitor


def solution(mesh):
    in_specs = (
        P("tile", None),
        P("src", None, None, None, None, None),
        P("src"),
        P("src"),
        P("src"),
    )
    out_specs = (P("src", "tile", None), P("src", "tile", None))
    return jax.shard_map(shards, mesh=mesh, in_specs=in_specs, out_specs=out_specs, check_vma=False)
```

```python
import jax
import jax.numpy as jnp
from jax import lax
from jax.experimental import pallas as pl
from jax.experimental.pallas import tpu as pltpu
from jax.sharding import PartitionSpec as P

STEPS = 8
KS = 17
TAPS = KS * KS
KPAD = 304
WCOL = 304
WLANES = 384
COLS = 512
TILES = COLS // 128
OWN = 16
HALF = 16
ROWS = OWN + 2 * STEPS
PLANES = 8
GROUPS = 4
PARAMS = 64

acid_lateral = 0.15
acid_vertical = 0.12
quench_lateral = 0.05
quench_vertical = 0.04
react_rate = 0.3
deprotect_rate = 0.25


def one_hot(axis):
    place = lax.broadcasted_iota(jnp.int32, (COLS, COLS), 1 - axis)
    column = lax.broadcasted_iota(jnp.int32, (COLS, COLS), axis)
    where_to = (place & 127) * TILES + (place >> 7)
    return jnp.where(where_to == column, 1.0, 0.0).astype(jnp.bfloat16)


def pack_kernel(taps_ref, weight_ref, out_ref):
    row = lax.broadcasted_iota(jnp.int32, (96, 128), 0)
    lane = lax.broadcasted_iota(jnp.int32, (96, 128), 1)
    source = (row // 6) & 3
    weight = jnp.zeros((96, 128), jnp.float32)
    for p in range(4):
        weight = jnp.where(source == p, weight_ref[p].astype(jnp.float32), weight)
    tail = jnp.where(lane == WCOL - 256, weight, 0.0).astype(jnp.bfloat16)
    for half in range(2):
        last = jnp.concatenate([taps_ref[half, :, 256:], tail[:, TAPS - 256 :]], axis=1)
        for part in (half, half + 2):
            out_ref[part, :, :256] = taps_ref[half, :, :256]
            out_ref[part, :, 256:] = last


def image_kernel(near_ref, mask_ref, w_ref, dill_ref, load_ref, out_ref, b_ref, i_ref):
    f32 = jnp.float32
    upper = lax.axis_index("src") < 2
    near, own = near_ref[...], mask_ref[...]
    band = jnp.concatenate([jnp.where(upper, near, own), jnp.where(upper, own, near)], axis=0)
    band = jnp.dot(band.astype(f32).astype(jnp.bfloat16), one_hot(0), preferred_element_type=f32)
    filled = 2 * HALF * KS
    b_ref[:, filled:, :] = jnp.zeros((TILES, b_ref.shape[1] - filled, 128), f32)
    lane = lax.broadcasted_iota(jnp.int32, (2 * HALF, 128), 1)
    moved = {}
    for m in range(-8, 12):
        tile, by = m % TILES, m // TILES
        block = band[:, 128 * tile : 128 * tile + 128]
        if by:
            block = pltpu.roll(block, (-by) % 128, 1)
            block = jnp.where((lane + by >= 0) & (lane + by < 128), block, 0.0)
        moved[m] = block
    for b in range(KS):
        for t in range(TILES):
            b_ref[t, pl.ds(b, 2 * HALF, stride=KS), :] = moved[t + b - 8]
    w_all = w_ref[...].reshape(384, WLANES)
    weight = w_all[:, WCOL : WCOL + 1].astype(f32)
    w_taps = w_all[:, :KPAD]

    def body(q, carry):
        base = pl.multiple_of(q * (8 * KS), 8)
        view = b_ref.at[:, pl.ds(base, 424), :]
        for d in range(8):
            patches = jnp.concatenate(
                [view[t, KS * d : KS * d + KPAD, :] for t in range(TILES)], axis=1
            ).astype(jnp.bfloat16)
            field = jnp.dot(w_taps, patches, preferred_element_type=f32)
            power = (field * field * weight).reshape(4, 4, 3, 8, COLS)
            total = power.sum(axis=(0, 2)).sum(axis=1)
            for k in range(4):
                at = k * HALF + (d % 4) * 4 + d // 4 + 2 * q
                i_ref[pl.ds(at, 1), :] = total[k : k + 1]
        return carry

    lax.fori_loop(0, HALF // 8, body, 0)
    i_ref[PARAMS:, :] = jnp.zeros((16, COLS), f32)
    at = PARAMS
    for ref in (dill_ref, load_ref):
        for k in range(2):
            rest = jnp.full((1, COLS), ref[k], f32)
            for _ in range(3):
                part = rest.astype(jnp.bfloat16).astype(f32)
                i_ref[at : at + 1, :] = part
                rest = rest - part
                at += 1
    out_ref[...] = i_ref[...].astype(jnp.bfloat16)


def bake_kernel(scale, g_ref, acid_ref, inhib_ref, a0_ref, a1_ref, q0_ref, q1_ref, d_ref):
    f32 = jnp.float32
    tile = lax.axis_index("tile")
    src = lax.axis_index("src")
    lane = lax.broadcasted_iota(jnp.int32, (8, 128), 1)
    sub = lax.broadcasted_iota(jnp.int32, (8, 128), 0)
    has_up = jnp.where(tile > 0, 1.0, 0.0).astype(f32)
    has_down = jnp.where(tile < lax.axis_size("tile") - 1, 1.0, 0.0).astype(f32)
    keep = jnp.where(sub < 2, has_up, jnp.where(sub >= 6, has_down, 1.0))
    top = sub < 4
    scaled = keep * react_rate
    for k in range(PLANES):
        par = g_ref[k // 2, PARAMS : PARAMS + 16, 0:128].astype(f32)

        def constant(at):
            return jnp.broadcast_to(par[at : at + 1] + par[at + 1 : at + 2] + par[at + 2 : at + 3], (8, 128))

        dill = constant(3 * (k % 2)) * -scale
        load = constant(6 + 3 * (k % 2)) * scaled
        first = (k % 4) * HALF
        for t in range(TILES):
            cut = slice(128 * t, 128 * t + 128)
            high = g_ref[k // 4, first : first + HALF, cut].astype(f32)
            low = g_ref[k // 4 + 2, first : first + HALF, cut].astype(f32)
            for half in range(2):
                one, two = high[8 * half : 8 * half + 8], low[8 * half : 8 * half + 8]
                pair = (jnp.where(top, one, pltpu.roll(two, 4, 0)), jnp.where(top, pltpu.roll(one, 4, 0), two))
                for i in range(2):
                    at = (2 * half + i) * TILES + t
                    a0_ref[k, at] = (1.0 - jnp.exp(dill * pair[i])) * scaled
                    q0_ref[k, at] = load

    not_first, not_last = lane > 0, lane < 127
    acid_keep = keep * (1.0 - 4.0 * acid_lateral - 2.0 * acid_vertical)
    load_keep = keep * (1.0 - 4.0 * quench_lateral - 2.0 * quench_vertical)
    acid_side, acid_up = keep * acid_lateral, keep * acid_vertical
    load_side, load_up = keep * quench_lateral, keep * quench_vertical

    def around(ref, k, here):
        under, over = jnp.maximum(k - 1, 0), jnp.minimum(k + 1, PLANES - 1)
        side, vertical = [], []
        for u in range(GROUPS):
            for t in range(TILES):
                at = u * TILES + t
                above = here[at - TILES] if u > 0 else pltpu.roll(here[at + 3 * TILES], 1, 0)
                below = here[at + TILES] if u < GROUPS - 1 else pltpu.roll(here[at - 3 * TILES], 7, 0)
                left = here[at - 1] if t > 0 else jnp.where(not_first, pltpu.roll(here[at + 3], 1, 1), 0.0)
                right = here[at + 1] if t < TILES - 1 else jnp.where(not_last, pltpu.roll(here[at - 3], 127, 1), 0.0)
                side.append((above + below) + (left + right))
                vertical.append(ref[under, at] + ref[over, at])
        return side, vertical

    for step in range(STEPS):
        a_now, a_new = (a0_ref, a1_ref) if step % 2 == 0 else (a1_ref, a0_ref)
        q_now, q_new = (q0_ref, q1_ref) if step % 2 == 0 else (q1_ref, q0_ref)
        reach = STEPS - 1 - step

        low = jnp.maximum(2 * src - reach, 0)
        count = (jnp.minimum(2 * src + 1 + reach, PLANES - 1) + 2 - low) // 2
        low = jnp.minimum(low, PLANES - 2 * count)

        def body(i, carry):
            for j in range(2):
                plane(low + 2 * i + j)
            return carry

        def plane(k):
            acid = [a_now[k, at] for at in range(16)]
            load = [q_now[k, at] for at in range(16)]
            a_side, a_up = around(a_now, k, acid)
            q_side, q_up = around(q_now, k, load)
            for at in range(16):
                reacted = acid[at] * load[at]
                a_new[k, at] = (acid_keep * acid[at] + acid_side * a_side[at]) + (acid_up * a_up[at] - reacted)
                q_new[k, at] = (load_keep * load[at] + load_side * q_side[at]) + (load_up * q_up[at] - reacted)

        lax.fori_loop(0, count, body, 0)
        for k in range(2):
            for at in range(16):
                value = a_new[2 * src + k, at]
                d_ref[k, at] = value if step == 0 else d_ref[k, at] + value

    blocks = []
    for k in range(2):
        for u in range(GROUPS):
            blocks.append(jnp.concatenate([a_new[2 * src + k, u * TILES + t] for t in range(TILES)], axis=1))
    for k in range(2):
        for u in range(GROUPS):
            blocks.append(jnp.concatenate([d_ref[k, u * TILES + t] for t in range(TILES)], axis=1))
    rest = jnp.concatenate(blocks, axis=0)
    back = one_hot(1)
    result = None
    for _ in range(3):
        part = rest.astype(jnp.bfloat16)
        rest = rest - part.astype(f32)
        moved = jnp.dot(part, back, preferred_element_type=f32)
        result = moved if result is None else result + moved
    inhibitor = jnp.exp((-deprotect_rate / react_rate) * result[64:])
    acid_out = result[:64] * (1.0 / react_rate)
    for k in range(2):
        for u in range(GROUPS):
            for j in range(2, 6):
                row = 32 * k + 8 * u + j
                to = 4 * (j - 2) + u
                acid_ref[k, to : to + 1, :] = acid_out[row : row + 1]
                inhib_ref[k, to : to + 1, :] = inhibitor[row : row + 1]


def bake_scratch():
    state = pltpu.VMEM((PLANES, 16, 8, 128), jnp.float32)
    return [state, state, state, state, pltpu.VMEM((2, 16, 8, 128), jnp.float32)]

def shards(mask_tiles, kernels, source_weight, dill_rate, quencher_load):
    bf16 = jnp.bfloat16
    tiles, parts = lax.axis_size("tile"), lax.axis_size("src")
    sources = kernels.shape[0]
    moves = []
    for i in range(tiles - 1):
        for s in range(parts):
            one, two = i * parts + s, (i + 1) * parts + s
            moves.append((one, two) if s < 2 else (two, one))
    near = lax.ppermute(mask_tiles, ("tile", "src"), moves)

    taps = kernels.reshape(sources, 3, 2, 4, 2, KS, KS).transpose(2, 3, 0, 1, 4, 5, 6).reshape(2, 96, TAPS)
    smem = pl.BlockSpec(memory_space=pltpu.SMEM)
    vmem = pl.BlockSpec(memory_space=pltpu.VMEM)
    packed = pl.pallas_call(
        pack_kernel,
        out_shape=jax.ShapeDtypeStruct((parts, 96, WLANES), bf16),
        in_specs=[vmem, smem],
        out_specs=vmem,
        compiler_params=pltpu.CompilerParams(vmem_limit_bytes=16 * 1024 * 1024),
        name="pack",
    )(taps, source_weight)
    w_own = lax.all_to_all(packed, "src", 0, 0)

    intensity = pl.pallas_call(
        image_kernel,
        out_shape=jax.ShapeDtypeStruct((PARAMS + 16, COLS), bf16),
        in_specs=[vmem, vmem, vmem, smem, smem],
        scratch_shapes=[
            pltpu.VMEM((TILES, 560, 128), jnp.float32),
            pltpu.VMEM((PARAMS + 16, COLS), jnp.float32),
        ],
        compiler_params=pltpu.CompilerParams(vmem_limit_bytes=16 * 1024 * 1024),
        name="image",
    )(near, mask_tiles, w_own, dill_rate, quencher_load)
    gathered = lax.all_gather(intensity, "src")
    scale = 1.0 / (24.0 * sources * parts)

    def bake(*refs):
        bake_kernel(scale, *refs)

    out = jax.ShapeDtypeStruct((2, OWN, COLS), jnp.float32)
    acid, inhibitor = pl.pallas_call(
        bake,
        out_shape=(out, out),
        scratch_shapes=bake_scratch(),
        compiler_params=pltpu.CompilerParams(vmem_limit_bytes=16 * 1024 * 1024),
        name="bake",
    )(gathered)
    return acid, inhibitor


def solution(mesh):
    in_specs = (
        P("tile", None),
        P("src", None, None, None, None, None),
        P("src"),
        P("src"),
        P("src"),
    )
    out_specs = (P("src", "tile", None), P("src", "tile", None))
    return jax.shard_map(shards, mesh=mesh, in_specs=in_specs, out_specs=out_specs, check_vma=False)
```

```python
import jax
import jax.numpy as jnp
from jax import lax
from jax.experimental import pallas as pl
from jax.experimental.pallas import tpu as pltpu
from jax.sharding import PartitionSpec as P

STEPS = 8
KS = 17
TAPS = KS * KS
KPAD = 304
WCOL = 304
WLANES = 384
COLS = 512
TILES = COLS // 128
OWN = 16
HALF = 16
ROWS = OWN + 2 * STEPS
PLANES = 8
GROUPS = 4
PARAMS = 64

acid_lateral = 0.15
acid_vertical = 0.12
quench_lateral = 0.05
quench_vertical = 0.04
react_rate = 0.3
deprotect_rate = 0.25


def one_hot(axis):
    place = lax.broadcasted_iota(jnp.int32, (COLS, COLS), 1 - axis)
    column = lax.broadcasted_iota(jnp.int32, (COLS, COLS), axis)
    where_to = (place & 127) * TILES + (place >> 7)
    return jnp.where(where_to == column, 1.0, 0.0).astype(jnp.bfloat16)


def image_kernel(near_ref, mask_ref, w_ref, dill_ref, load_ref, out_ref, b_ref, i_ref):
    f32 = jnp.float32
    upper = lax.axis_index("src") < 2
    near, own = near_ref[...], mask_ref[...]
    band = jnp.concatenate([jnp.where(upper, near, own), jnp.where(upper, own, near)], axis=0)
    band = jnp.dot(band.astype(f32).astype(jnp.bfloat16), one_hot(0), preferred_element_type=f32)
    filled = 2 * HALF * KS
    b_ref[:, filled:, :] = jnp.zeros((TILES, b_ref.shape[1] - filled, 128), f32)
    lane = lax.broadcasted_iota(jnp.int32, (2 * HALF, 128), 1)
    moved = {}
    for m in range(-8, 12):
        tile, by = m % TILES, m // TILES
        block = band[:, 128 * tile : 128 * tile + 128]
        if by:
            block = pltpu.roll(block, (-by) % 128, 1)
            block = jnp.where((lane + by >= 0) & (lane + by < 128), block, 0.0)
        moved[m] = block
    for b in range(KS):
        for t in range(TILES):
            b_ref[t, pl.ds(b, 2 * HALF, stride=KS), :] = moved[t + b - 8]
    w_all = w_ref[...].reshape(384, WLANES)
    weight = w_all[:, WCOL : WCOL + 1].astype(f32)
    w_taps = w_all[:, :KPAD]

    def body(q, carry):
        base = pl.multiple_of(q * (8 * KS), 8)
        view = b_ref.at[:, pl.ds(base, 424), :]
        for d in range(8):
            patches = jnp.concatenate(
                [view[t, KS * d : KS * d + KPAD, :] for t in range(TILES)], axis=1
            ).astype(jnp.bfloat16)
            field = jnp.dot(w_taps, patches, preferred_element_type=f32)
            power = (field * field * weight).reshape(4, 4, 3, 8, COLS)
            total = power.sum(axis=(0, 2)).sum(axis=1)
            for k in range(4):
                at = k * HALF + (d % 4) * 4 + d // 4 + 2 * q
                i_ref[pl.ds(at, 1), :] = total[k : k + 1]
        return carry

    lax.fori_loop(0, HALF // 8, body, 0)
    i_ref[PARAMS:, :] = jnp.zeros((16, COLS), f32)
    at = PARAMS
    for ref in (dill_ref, load_ref):
        for k in range(2):
            rest = jnp.full((1, COLS), ref[k], f32)
            for _ in range(3):
                part = rest.astype(jnp.bfloat16).astype(f32)
                i_ref[at : at + 1, :] = part
                rest = rest - part
                at += 1
    out_ref[...] = i_ref[...].astype(jnp.bfloat16)


def bake_kernel(scale, g_ref, acid_ref, inhib_ref, a0_ref, a1_ref, q0_ref, q1_ref, d_ref):
    f32 = jnp.float32
    tile = lax.axis_index("tile")
    src = lax.axis_index("src")
    lane = lax.broadcasted_iota(jnp.int32, (8, 128), 1)
    sub = lax.broadcasted_iota(jnp.int32, (8, 128), 0)
    has_up = jnp.where(tile > 0, 1.0, 0.0).astype(f32)
    has_down = jnp.where(tile < lax.axis_size("tile") - 1, 1.0, 0.0).astype(f32)
    keep = jnp.where(sub < 2, has_up, jnp.where(sub >= 6, has_down, 1.0))
    top = sub < 4
    scaled = keep * react_rate
    for k in range(PLANES):
        par = g_ref[k // 2, PARAMS : PARAMS + 16, 0:128].astype(f32)

        def constant(at):
            return jnp.broadcast_to(par[at : at + 1] + par[at + 1 : at + 2] + par[at + 2 : at + 3], (8, 128))

        dill = constant(3 * (k % 2)) * -scale
        load = constant(6 + 3 * (k % 2)) * scaled
        first = (k % 4) * HALF
        for t in range(TILES):
            cut = slice(128 * t, 128 * t + 128)
            high = g_ref[k // 4, first : first + HALF, cut].astype(f32)
            low = g_ref[k // 4 + 2, first : first + HALF, cut].astype(f32)
            for half in range(2):
                one, two = high[8 * half : 8 * half + 8], low[8 * half : 8 * half + 8]
                pair = (jnp.where(top, one, pltpu.roll(two, 4, 0)), jnp.where(top, pltpu.roll(one, 4, 0), two))
                for i in range(2):
                    at = (2 * half + i) * TILES + t
                    a0_ref[k, at] = (1.0 - jnp.exp(dill * pair[i])) * scaled
                    q0_ref[k, at] = load

    not_first, not_last = lane > 0, lane < 127
    acid_keep = keep * (1.0 - 4.0 * acid_lateral - 2.0 * acid_vertical)
    load_keep = keep * (1.0 - 4.0 * quench_lateral - 2.0 * quench_vertical)
    acid_side, acid_up = keep * acid_lateral, keep * acid_vertical
    load_side, load_up = keep * quench_lateral, keep * quench_vertical

    def around(ref, k, here):
        under, over = jnp.maximum(k - 1, 0), jnp.minimum(k + 1, PLANES - 1)
        side, vertical = [], []
        for u in range(GROUPS):
            for t in range(TILES):
                at = u * TILES + t
                above = here[at - TILES] if u > 0 else pltpu.roll(here[at + 3 * TILES], 1, 0)
                below = here[at + TILES] if u < GROUPS - 1 else pltpu.roll(here[at - 3 * TILES], 7, 0)
                left = here[at - 1] if t > 0 else jnp.where(not_first, pltpu.roll(here[at + 3], 1, 1), 0.0)
                right = here[at + 1] if t < TILES - 1 else jnp.where(not_last, pltpu.roll(here[at - 3], 127, 1), 0.0)
                side.append((above + below) + (left + right))
                vertical.append(ref[under, at] + ref[over, at])
        return side, vertical

    for step in range(STEPS):
        a_now, a_new = (a0_ref, a1_ref) if step % 2 == 0 else (a1_ref, a0_ref)
        q_now, q_new = (q0_ref, q1_ref) if step % 2 == 0 else (q1_ref, q0_ref)
        reach = STEPS - 1 - step

        low = jnp.maximum(2 * src - reach, 0)
        count = (jnp.minimum(2 * src + 1 + reach, PLANES - 1) + 2 - low) // 2
        low = jnp.minimum(low, PLANES - 2 * count)

        def body(i, carry):
            for j in range(2):
                plane(low + 2 * i + j)
            return carry

        def plane(k):
            acid = [a_now[k, at] for at in range(16)]
            load = [q_now[k, at] for at in range(16)]
            a_side, a_up = around(a_now, k, acid)
            q_side, q_up = around(q_now, k, load)
            for at in range(16):
                reacted = acid[at] * load[at]
                a_new[k, at] = (acid_keep * acid[at] + acid_side * a_side[at]) + (acid_up * a_up[at] - reacted)
                q_new[k, at] = (load_keep * load[at] + load_side * q_side[at]) + (load_up * q_up[at] - reacted)

        lax.fori_loop(0, count, body, 0)
        for k in range(2):
            for at in range(16):
                value = a_new[2 * src + k, at]
                d_ref[k, at] = value if step == 0 else d_ref[k, at] + value

    blocks = []
    for k in range(2):
        for u in range(GROUPS):
            blocks.append(jnp.concatenate([a_new[2 * src + k, u * TILES + t] for t in range(TILES)], axis=1))
    for k in range(2):
        for u in range(GROUPS):
            blocks.append(jnp.concatenate([d_ref[k, u * TILES + t] for t in range(TILES)], axis=1))
    rest = jnp.concatenate(blocks, axis=0)
    back = one_hot(1)
    result = None
    for _ in range(3):
        part = rest.astype(jnp.bfloat16)
        rest = rest - part.astype(f32)
        moved = jnp.dot(part, back, preferred_element_type=f32)
        result = moved if result is None else result + moved
    inhibitor = jnp.exp((-deprotect_rate / react_rate) * result[64:])
    acid_out = result[:64] * (1.0 / react_rate)
    for k in range(2):
        for u in range(GROUPS):
            for j in range(2, 6):
                row = 32 * k + 8 * u + j
                to = 4 * (j - 2) + u
                acid_ref[k, to : to + 1, :] = acid_out[row : row + 1]
                inhib_ref[k, to : to + 1, :] = inhibitor[row : row + 1]


def bake_scratch():
    state = pltpu.VMEM((PLANES, 16, 8, 128), jnp.float32)
    return [state, state, state, state, pltpu.VMEM((2, 16, 8, 128), jnp.float32)]

def shards(mask_tiles, kernels, source_weight, dill_rate, quencher_load):
    bf16 = jnp.bfloat16
    tiles, parts = lax.axis_size("tile"), lax.axis_size("src")
    sources = kernels.shape[0]
    moves = []
    for i in range(tiles - 1):
        for s in range(parts):
            one, two = i * parts + s, (i + 1) * parts + s
            moves.append((one, two) if s < 2 else (two, one))
    near = lax.ppermute(mask_tiles, ("tile", "src"), moves)

    shape = (KS, KS, WLANES)
    tap = lax.broadcasted_iota(jnp.int32, shape, 0) * KS + lax.broadcasted_iota(jnp.int32, shape, 1)
    places = (lax.broadcasted_iota(jnp.int32, shape, 2) == tap).astype(bf16)
    split = kernels.reshape(sources, 3, 2, 4, 2, KS, KS)
    taps = jnp.einsum("pchkqab,abj->hkpcqj", split, places, preferred_element_type=bf16)
    behind = lax.broadcasted_iota(jnp.int32, (1, 1, 1, 1, 1, WLANES), 5) == WCOL
    taps = taps + jnp.where(behind, source_weight.astype(bf16).reshape(1, 1, sources, 1, 1, 1), 0)
    packed = jnp.broadcast_to(taps[None], (2,) + taps.shape).reshape(parts, 96, WLANES)
    w_own = lax.all_to_all(packed, "src", 0, 0)

    smem = pl.BlockSpec(memory_space=pltpu.SMEM)
    vmem = pl.BlockSpec(memory_space=pltpu.VMEM)
    intensity = pl.pallas_call(
        image_kernel,
        out_shape=jax.ShapeDtypeStruct((PARAMS + 16, COLS), bf16),
        in_specs=[vmem, vmem, vmem, smem, smem],
        scratch_shapes=[
            pltpu.VMEM((TILES, 560, 128), jnp.float32),
            pltpu.VMEM((PARAMS + 16, COLS), jnp.float32),
        ],
        compiler_params=pltpu.CompilerParams(vmem_limit_bytes=16 * 1024 * 1024),
        name="image",
    )(near, mask_tiles, w_own, dill_rate, quencher_load)
    gathered = lax.all_gather(intensity, "src")
    scale = 1.0 / (24.0 * sources * parts)

    def bake(*refs):
        bake_kernel(scale, *refs)

    out = jax.ShapeDtypeStruct((2, OWN, COLS), jnp.float32)
    acid, inhibitor = pl.pallas_call(
        bake,
        out_shape=(out, out),
        scratch_shapes=bake_scratch(),
        compiler_params=pltpu.CompilerParams(vmem_limit_bytes=16 * 1024 * 1024),
        name="bake",
    )(gathered)
    return acid, inhibitor


def solution(mesh):
    in_specs = (
        P("tile", None),
        P("src", None, None, None, None, None),
        P("src"),
        P("src"),
        P("src"),
    )
    out_specs = (P("src", "tile", None), P("src", "tile", None))
    return jax.shard_map(shards, mesh=mesh, in_specs=in_specs, out_specs=out_specs, check_vma=False)
```

```python
import jax
import jax.numpy as jnp
from jax import lax
from jax.experimental import pallas as pl
from jax.experimental.pallas import tpu as pltpu
from jax.sharding import PartitionSpec as P

STEPS = 8
KS = 17
TAPS = KS * KS
KPAD = 304
WCOL = 304
WLANES = 384
COLS = 512
TILES = COLS // 128
OWN = 16
HALF = 16
ROWS = OWN + 2 * STEPS
PLANES = 8
GROUPS = 4
PARAMS = 64
BAND_FLOPS = 1 << 34
BAND_BYTES = 1 << 26

acid_lateral = 0.15
acid_vertical = 0.12
quench_lateral = 0.05
quench_vertical = 0.04
react_rate = 0.3
deprotect_rate = 0.25


def one_hot(axis):
    place = lax.broadcasted_iota(jnp.int32, (COLS, COLS), 1 - axis)
    column = lax.broadcasted_iota(jnp.int32, (COLS, COLS), axis)
    where_to = (place & 127) * TILES + (place >> 7)
    return jnp.where(where_to == column, 1.0, 0.0).astype(jnp.bfloat16)


def band_kernel(near_ref, mask_ref, b_ref):
    f32 = jnp.float32
    upper = lax.axis_index("src") < 2
    near, own = near_ref[...], mask_ref[...]
    band = jnp.concatenate([jnp.where(upper, near, own), jnp.where(upper, own, near)], axis=0)
    band = jnp.dot(band.astype(f32).astype(jnp.bfloat16), one_hot(0), preferred_element_type=f32)
    filled = 2 * HALF * KS
    b_ref[:, filled:, :] = jnp.zeros((TILES, b_ref.shape[1] - filled, 128), f32)
    lane = lax.broadcasted_iota(jnp.int32, (2 * HALF, 128), 1)
    moved = {}
    for m in range(-8, 12):
        tile, by = m % TILES, m // TILES
        block = band[:, 128 * tile : 128 * tile + 128]
        if by:
            block = pltpu.roll(block, (-by) % 128, 1)
            block = jnp.where((lane + by >= 0) & (lane + by < 128), block, 0.0)
        moved[m] = block
    for b in range(KS):
        for t in range(TILES):
            b_ref[t, pl.ds(b, 2 * HALF, stride=KS), :] = moved[t + b - 8]


def image_kernel(b_ref, *refs):
    f32 = jnp.float32
    own_ref, near_e, far_e, *late = refs[:6]
    dill_ref, load_ref, out_ref, i_ref = refs[6:]
    early = [near_e[...], far_e[0], far_e[1]]
    w_all = jnp.concatenate([own_ref[...]] + [e + l[...] for e, l in zip(early, late)], axis=0)
    weight = w_all[:, WCOL : WCOL + 1].astype(f32)
    w_taps = w_all[:, :KPAD]

    def body(q, carry):
        base = pl.multiple_of(q * (8 * KS), 8)
        view = b_ref.at[:, pl.ds(base, 424), :]
        for d in range(8):
            patches = jnp.concatenate(
                [view[t, KS * d : KS * d + KPAD, :] for t in range(TILES)], axis=1
            ).astype(jnp.bfloat16)
            field = jnp.dot(w_taps, patches, preferred_element_type=f32)
            power = (field * field * weight).reshape(4, 4, 3, 8, COLS)
            total = power.sum(axis=(0, 2)).sum(axis=1)
            for k in range(4):
                at = k * HALF + (d % 4) * 4 + d // 4 + 2 * q
                i_ref[pl.ds(at, 1), :] = total[k : k + 1]
        return carry

    lax.fori_loop(0, HALF // 8, body, 0)
    i_ref[PARAMS:, :] = jnp.zeros((16, COLS), f32)
    at = PARAMS
    for ref in (dill_ref, load_ref):
        for k in range(2):
            rest = jnp.full((1, COLS), ref[k], f32)
            for _ in range(3):
                part = rest.astype(jnp.bfloat16).astype(f32)
                i_ref[at : at + 1, :] = part
                rest = rest - part
                at += 1
    out_ref[...] = i_ref[...].astype(jnp.bfloat16)


def bake_kernel(scale, g_ref, acid_ref, inhib_ref, a0_ref, a1_ref, q0_ref, q1_ref, d_ref):
    f32 = jnp.float32
    tile = lax.axis_index("tile")
    src = lax.axis_index("src")
    lane = lax.broadcasted_iota(jnp.int32, (8, 128), 1)
    sub = lax.broadcasted_iota(jnp.int32, (8, 128), 0)
    has_up = jnp.where(tile > 0, 1.0, 0.0).astype(f32)
    has_down = jnp.where(tile < lax.axis_size("tile") - 1, 1.0, 0.0).astype(f32)
    keep = jnp.where(sub < 2, has_up, jnp.where(sub >= 6, has_down, 1.0))
    top = sub < 4
    scaled = keep * react_rate
    for k in range(PLANES):
        par = g_ref[k // 2, PARAMS : PARAMS + 16, 0:128].astype(f32)

        def constant(at):
            return jnp.broadcast_to(par[at : at + 1] + par[at + 1 : at + 2] + par[at + 2 : at + 3], (8, 128))

        dill = constant(3 * (k % 2)) * -scale
        load = constant(6 + 3 * (k % 2)) * scaled
        first = (k % 4) * HALF
        for t in range(TILES):
            cut = slice(128 * t, 128 * t + 128)
            high = g_ref[k // 4, first : first + HALF, cut].astype(f32)
            low = g_ref[k // 4 + 2, first : first + HALF, cut].astype(f32)
            for half in range(2):
                one, two = high[8 * half : 8 * half + 8], low[8 * half : 8 * half + 8]
                pair = (jnp.where(top, one, pltpu.roll(two, 4, 0)), jnp.where(top, pltpu.roll(one, 4, 0), two))
                for i in range(2):
                    at = (2 * half + i) * TILES + t
                    a0_ref[k, at] = (1.0 - jnp.exp(dill * pair[i])) * scaled
                    q0_ref[k, at] = load

    not_first, not_last = lane > 0, lane < 127
    acid_keep = keep * (1.0 - 4.0 * acid_lateral - 2.0 * acid_vertical)
    load_keep = keep * (1.0 - 4.0 * quench_lateral - 2.0 * quench_vertical)
    acid_side, acid_up = keep * acid_lateral, keep * acid_vertical
    load_side, load_up = keep * quench_lateral, keep * quench_vertical

    def around(ref, k, here):
        under, over = jnp.maximum(k - 1, 0), jnp.minimum(k + 1, PLANES - 1)
        side, vertical = [], []
        for u in range(GROUPS):
            for t in range(TILES):
                at = u * TILES + t
                above = here[at - TILES] if u > 0 else pltpu.roll(here[at + 3 * TILES], 1, 0)
                below = here[at + TILES] if u < GROUPS - 1 else pltpu.roll(here[at - 3 * TILES], 7, 0)
                left = here[at - 1] if t > 0 else jnp.where(not_first, pltpu.roll(here[at + 3], 1, 1), 0.0)
                right = here[at + 1] if t < TILES - 1 else jnp.where(not_last, pltpu.roll(here[at - 3], 127, 1), 0.0)
                side.append((above + below) + (left + right))
                vertical.append(ref[under, at] + ref[over, at])
        return side, vertical

    for step in range(STEPS):
        a_now, a_new = (a0_ref, a1_ref) if step % 2 == 0 else (a1_ref, a0_ref)
        q_now, q_new = (q0_ref, q1_ref) if step % 2 == 0 else (q1_ref, q0_ref)
        reach = STEPS - 1 - step

        low = jnp.maximum(2 * src - reach, 0)
        count = (jnp.minimum(2 * src + 1 + reach, PLANES - 1) + 2 - low) // 2
        low = jnp.minimum(low, PLANES - 2 * count)

        def body(i, carry):
            for j in range(2):
                plane(low + 2 * i + j)
            return carry

        def plane(k):
            acid = [a_now[k, at] for at in range(16)]
            load = [q_now[k, at] for at in range(16)]
            a_side, a_up = around(a_now, k, acid)
            q_side, q_up = around(q_now, k, load)
            for at in range(16):
                reacted = acid[at] * load[at]
                a_new[k, at] = (acid_keep * acid[at] + acid_side * a_side[at]) + (acid_up * a_up[at] - reacted)
                q_new[k, at] = (load_keep * load[at] + load_side * q_side[at]) + (load_up * q_up[at] - reacted)

        lax.fori_loop(0, count, body, 0)
        for k in range(2):
            for at in range(16):
                value = a_new[2 * src + k, at]
                d_ref[k, at] = value if step == 0 else d_ref[k, at] + value

    blocks = []
    for k in range(2):
        for u in range(GROUPS):
            blocks.append(jnp.concatenate([a_new[2 * src + k, u * TILES + t] for t in range(TILES)], axis=1))
    for k in range(2):
        for u in range(GROUPS):
            blocks.append(jnp.concatenate([d_ref[k, u * TILES + t] for t in range(TILES)], axis=1))
    rest = jnp.concatenate(blocks, axis=0)
    back = one_hot(1)
    result = None
    for _ in range(3):
        part = rest.astype(jnp.bfloat16)
        rest = rest - part.astype(f32)
        moved = jnp.dot(part, back, preferred_element_type=f32)
        result = moved if result is None else result + moved
    inhibitor = jnp.exp((-deprotect_rate / react_rate) * result[64:])
    acid_out = result[:64] * (1.0 / react_rate)
    for k in range(2):
        for u in range(GROUPS):
            for j in range(2, 6):
                row = 32 * k + 8 * u + j
                to = 4 * (j - 2) + u
                acid_ref[k, to : to + 1, :] = acid_out[row : row + 1]
                inhib_ref[k, to : to + 1, :] = inhibitor[row : row + 1]


def bake_scratch():
    state = pltpu.VMEM((PLANES, 16, 8, 128), jnp.float32)
    return [state, state, state, state, pltpu.VMEM((2, 16, 8, 128), jnp.float32)]

def shards(mask_tiles, kernels, source_weight, dill_rate, quencher_load):
    bf16 = jnp.bfloat16
    tiles, parts = lax.axis_size("tile"), lax.axis_size("src")
    sources = kernels.shape[0]
    moves = []
    for i in range(tiles - 1):
        for s in range(parts):
            one, two = i * parts + s, (i + 1) * parts + s
            moves.append((one, two) if s < 2 else (two, one))
    near = lax.ppermute(mask_tiles, ("tile", "src"), moves)

    lane = lax.broadcasted_iota(jnp.int32, (KS, KS, WLANES), 2)
    tap = lax.broadcasted_iota(jnp.int32, (KS, KS, WLANES), 0) * KS + lax.broadcasted_iota(jnp.int32, (KS, KS, WLANES), 1)
    places = (lane == tap).astype(bf16)
    split = kernels.reshape(sources, 3, 2, 4, 2, KS, KS)
    taps = jnp.einsum("pchkqab,abj->hkpcqj", split, places, preferred_element_type=bf16)
    behind = lax.broadcasted_iota(jnp.int32, (1, 1, 1, 1, 1, WLANES), 5) == WCOL
    taps = taps + jnp.where(behind, source_weight.astype(bf16).reshape(1, 1, sources, 1, 1, 1), 0)
    taps = taps.reshape(2, 96, WLANES)
    odd = lax.axis_index("src") % 2 == 1
    same = jnp.where(odd, taps[1], taps[0])
    other = jnp.where(odd, taps[0], taps[1])

    def swap(block, late, bit):
        pairs = [
            (i * parts + s, i * parts + (s ^ bit))
            for i in range(tiles)
            if (i % 4 >= 2) == late
            for s in range(parts)
        ]
        return lax.ppermute(block, ("tile", "src"), pairs)

    near_e = swap(other, False, 1)
    far_e = swap(jnp.stack([same, near_e]), False, 2)
    same_later, other_later, near_e, far_e = lax.optimization_barrier((same, other, near_e, far_e))
    late = [swap(block, True, bit) for block, bit in ((other_later, 1), (same_later, 2), (other_later, 3))]

    smem = pl.BlockSpec(memory_space=pltpu.SMEM)
    vmem = pl.BlockSpec(memory_space=pltpu.VMEM)
    band = pl.pallas_call(
        band_kernel,
        out_shape=jax.ShapeDtypeStruct((TILES, 560, 128), jnp.float32),
        in_specs=[vmem, vmem],
        out_specs=vmem,
        compiler_params=pltpu.CompilerParams(vmem_limit_bytes=16 * 1024 * 1024),
        cost_estimate=pl.CostEstimate(flops=BAND_FLOPS, bytes_accessed=BAND_BYTES, transcendentals=0),
        name="band",
    )(near, mask_tiles)
    intensity = pl.pallas_call(
        image_kernel,
        out_shape=jax.ShapeDtypeStruct((PARAMS + 16, COLS), bf16),
        in_specs=[vmem] * 7 + [smem, smem],
        out_specs=vmem,
        scratch_shapes=[pltpu.VMEM((PARAMS + 16, COLS), jnp.float32)],
        compiler_params=pltpu.CompilerParams(vmem_limit_bytes=16 * 1024 * 1024),
        name="image",
    )(band, same, near_e, far_e, *late, dill_rate, quencher_load)
    gathered = lax.all_gather(intensity, "src")
    scale = 1.0 / (24.0 * sources * parts)

    def bake(*refs):
        bake_kernel(scale, *refs)

    out = jax.ShapeDtypeStruct((2, OWN, COLS), jnp.float32)
    acid, inhibitor = pl.pallas_call(
        bake,
        out_shape=(out, out),
        scratch_shapes=bake_scratch(),
        compiler_params=pltpu.CompilerParams(vmem_limit_bytes=16 * 1024 * 1024),
        name="bake",
    )(gathered)
    return acid, inhibitor


def solution(mesh):
    in_specs = (
        P("tile", None),
        P("src", None, None, None, None, None),
        P("src"),
        P("src"),
        P("src"),
    )
    out_specs = (P("src", "tile", None), P("src", "tile", None))
    return jax.shard_map(shards, mesh=mesh, in_specs=in_specs, out_specs=out_specs, check_vma=False)
```
